32 devices in a mesh: energy: 4 (over x, core), slab: 8 (over z, y).
Axes of the slice: x: 2, y: 2, z: 4, core: 2. Of those that a mesh axis runs over, the one named last changes fastest.
Arguments:
- g_lesser: bfloat16 [4, 8, 3, 2, 256, 256], P('energy', 'slab'), may hold values from -6 to 6
- g_greater: bfloat16 [4, 8, 3, 2, 256, 256], P('energy', 'slab'), may hold values from -6 to 6
- v_diag: bfloat16 [8, 2, 256, 256], P('slab'), may hold values from -0.15625 to 0.15625
- v_upper: bfloat16 [8, 2, 256, 256], P('slab'), may hold values from -0.15625 to 0.15625
Outputs:
- w_diag: bfloat16 [4, 8, 2, 256, 256], P('energy', 'slab')
- w_upper: bfloat16 [4, 8, 2, 256, 256], P('energy', 'slab')
The draws below stay inside these ranges and needn't reach their ends.
All inputs are finite; a program needn't handle non-finite values.
Results may differ from the reference program's by a relative error of at most 0.0058.
Values may be sent and summed in bfloat16 or wider, within the bound.
No kernel may reach another device: no remote copies, remote signals or barrier semaphores. Data moves between devices by JAX's collectives and lax.ppermute only.
A program may use at most 64 MiB of HBM per device.

```python
import math
import jax
import jax.numpy as jnp
from jax import lax

BS = 256
NE = 4
NB = 8


def levels(key, dims, cuts, smallest, high):
    def one(axis_at, blocks):
        draws = jax.random.uniform(jax.random.fold_in(jax.random.fold_in(key, 6), axis_at), (blocks,), jnp.float32, smallest / len(cuts), high / len(cuts))
        return jnp.repeat(jnp.exp(draws), dims[axis_at] // blocks).reshape((-1,) + (1,) * (len(dims) - axis_at - 1))

    factor_of = one(*cuts[0])
    for cut in cuts[1:]:
        factor_of = factor_of * one(*cut)
    return factor_of


def scatter_about(own_key, dims, deviation, reach, cuts=(), held_as=jnp.bfloat16):
    values = deviation * jax.random.normal(own_key, dims, jnp.float32)
    if cuts:
        values = values * levels(own_key, dims, cuts, -0.22, 0.18)
    return jnp.clip(values, -reach, reach).astype(held_as)


def setup_inputs(seed: int = 0) -> dict:
    streams_of = jax.random.split(jax.random.key(seed), 5)
    return {
        "g_lesser": scatter_about(streams_of[0], (NE, NB, 3, 2, BS, BS), 1.0, 6.0, ((0, 4), (1, 8))),
        "g_greater": scatter_about(streams_of[1], (NE, NB, 3, 2, BS, BS), 1.0, 6.0, ((0, 4), (1, 8))),
        "v_diag": scatter_about(streams_of[2], (NB, 2, BS, BS), (6 * BS) ** -0.5, 0.15625, ((0, 8),)),
        "v_upper": scatter_about(streams_of[3], (NB, 2, BS, BS), (6 * BS) ** -0.5, 0.15625, ((0, 8),)),
    }


def complex_product(left_block, right_block, left_adjoint=False, right_adjoint=False):
    left_re = left_block[..., 0, :, :].astype(jnp.float32)
    left_im = left_block[..., 1, :, :].astype(jnp.float32)
    right_re = right_block[..., 0, :, :].astype(jnp.float32)
    right_im = right_block[..., 1, :, :].astype(jnp.float32)
    pattern = ('...ji' if left_adjoint else '...ij') + ',' + ('...kj' if right_adjoint else '...jk') + '->...ik'

    def contract(first_part, second_part):
        return jnp.einsum(pattern, first_part, second_part, precision=lax.Precision.HIGHEST)
    left_sign = -1.0 if left_adjoint else 1.0
    right_sign = -1.0 if right_adjoint else 1.0
    real_part = contract(left_re, right_re) - left_sign * right_sign * contract(left_im, right_im)
    imag_part = right_sign * contract(left_re, right_im) + left_sign * contract(left_im, right_re)
    return jnp.stack([real_part, imag_part], axis=-3)

def screened(below_rows, middle, above_rows, diag_middle, diag_above, upper_below, upper_middle, upper_above):
    product = complex_product
    below_y = (product(below_rows[:, 1], upper_below) + product(below_rows[:, 2], diag_middle)).astype(jnp.bfloat16)
    below_z = product(below_rows[:, 2], upper_middle).astype(jnp.bfloat16)
    middle_y = (product(middle[:, 0], upper_below) + product(middle[:, 1], diag_middle) + product(middle[:, 2], upper_middle, False, True)).astype(jnp.bfloat16)
    middle_z = (product(middle[:, 1], upper_middle) + product(middle[:, 2], diag_above)).astype(jnp.bfloat16)
    above_y = (product(above_rows[:, 0], diag_middle) + product(above_rows[:, 1], upper_middle, False, True)).astype(jnp.bfloat16)
    above_z = (product(above_rows[:, 0], upper_middle) + product(above_rows[:, 1], diag_above) + product(above_rows[:, 2], upper_above, False, True)).astype(jnp.bfloat16)
    w_diag = (product(upper_below, below_y, True, False) + product(diag_middle, middle_y) + product(upper_middle, above_y)).astype(jnp.bfloat16)
    w_upper = (product(upper_below, below_z, True, False) + product(diag_middle, middle_z) + product(upper_middle, above_z)).astype(jnp.bfloat16)
    return (w_diag, w_upper)

def reference(g_lesser, g_greater, v_diag, v_upper):
    row_ids = jnp.arange(NB, dtype=jnp.int32)
    inside = (row_ids < NB - 1).astype(jnp.bfloat16)[:, None, None, None]
    upper_used = v_upper * inside
    zero_row = jnp.zeros_like(v_diag[:1])
    diag_padded = jnp.concatenate([zero_row, v_diag, zero_row], axis=0)
    upper_padded = jnp.concatenate([zero_row, upper_used, zero_row], axis=0)
    diag_middle = diag_padded[1:-1]
    diag_above = diag_padded[2:]
    upper_below = upper_padded[:-2]
    upper_middle = upper_padded[1:-1]
    upper_above = upper_padded[2:]
    factor = 1.0 / math.sqrt(NE)

    def one_energy(energy_out):

        def add_term(index, running):
            index = jnp.asarray(index).astype(jnp.int32)
            partner = (index - energy_out + NE // 2).astype(jnp.int32)
            inside_range = ((partner >= 0) & (partner < NE)).astype(jnp.float32)
            lesser = lax.dynamic_index_in_dim(g_lesser, index, 0, keepdims=False).astype(jnp.float32)
            greater = lax.dynamic_index_in_dim(g_greater, jnp.clip(partner, 0, NE - 1).astype(jnp.int32), 0, keepdims=False).astype(jnp.float32) * inside_range
            lesser_re = lesser[:, :, 0]
            lesser_im = lesser[:, :, 1]
            greater_re = greater[:, :, 0]
            greater_im = greater[:, :, 1]
            return running + jnp.stack([lesser_re * greater_im - lesser_im * greater_re, lesser_re * greater_re + lesser_im * greater_im], axis=2)
        summed = lax.fori_loop(0, NE, add_term, jnp.zeros((NB, 3, 2, BS, BS), jnp.float32))
        polarization = (summed * factor).astype(jnp.bfloat16)
        zero_band = jnp.zeros_like(polarization[:1])
        polar_padded = jnp.concatenate([zero_band, polarization, zero_band], axis=0)
        return screened(polar_padded[:-2], polarization, polar_padded[2:], diag_middle, diag_above, upper_below, upper_middle, upper_above)
    results = lax.map(one_energy, jnp.arange(NE, dtype=jnp.int32))
    return (results[0], results[1])
```

```python
import math

import jax
import jax.numpy as jnp
from jax import lax
from jax.experimental import pallas as pl
from jax.experimental.pallas import tpu as pltpu
from jax.sharding import PartitionSpec as P


def extended(shard, sides, width):
    for axis, dim in sides:
        count, length = (lax.axis_size(axis), shard.shape[dim])
        up = [(i, (i + 1) % count) for i in range(count - 1)]
        down = [(j, i) for i, j in up]
        last = lax.slice_in_dim(shard, length - width, length, axis=dim)
        initial = lax.slice_in_dim(shard, 0, width, axis=dim)
        before = lax.ppermute(last, axis, up)
        after = lax.ppermute(initial, axis, down)
        shard = jnp.concatenate([before, shard, after], axis=dim)
    return shard


def passed_along(value, axis, steps):
    count = lax.axis_size(axis)
    initial, last = (max(0, -steps), min(count, count - steps))
    return lax.ppermute(value, axis, [(source, source + steps) for source in range(initial, last)])


def complex_product(left_block, right_block, left_adjoint=False, right_adjoint=False):
    left_re = left_block[..., 0, :, :]
    left_im = left_block[..., 1, :, :]
    right_re = right_block[..., 0, :, :]
    right_im = right_block[..., 1, :, :]
    pattern = (
        ("...ji" if left_adjoint else "...ij")
        + ","
        + ("...kj" if right_adjoint else "...jk")
        + "->...ik"
    )

    def contract(first_part, second_part):
        return jnp.einsum(pattern, first_part, second_part, preferred_element_type=jnp.float32)

    left_sign = -1.0 if left_adjoint else 1.0
    right_sign = -1.0 if right_adjoint else 1.0
    real_part = contract(left_re, right_re) - left_sign * right_sign * contract(left_im, right_im)
    imag_part = right_sign * contract(left_re, right_im) + left_sign * contract(left_im, right_re)
    return jnp.stack([real_part, imag_part], axis=-3)


def transform(table, signal):
    return jnp.einsum("fn,n...->f...", table, signal, precision=lax.Precision.HIGH)


def correlate(pieces):
    lesser, greater = pieces
    energies = lesser.shape[0]
    length = 2 * energies
    frequency = jnp.arange(length, dtype=jnp.int32)
    energy_ids = jnp.arange(energies, dtype=jnp.int32)
    step_angle = 2.0 * math.pi / length
    forward_angle = (frequency[:, None] * energy_ids[None, :] % length).astype(
        jnp.float32
    ) * step_angle
    shifts = energy_ids - energies // 2
    inverse_angle = (shifts[:, None] * frequency[None, :] % length).astype(jnp.float32) * step_angle
    forward_cos = jnp.cos(forward_angle)
    forward_sin = jnp.sin(forward_angle)
    inverse_cos = jnp.cos(inverse_angle)
    inverse_sin = jnp.sin(inverse_angle)

    def spectrum(signal):
        signal_re = signal[:, :, :, 0].astype(jnp.float32)
        signal_im = signal[:, :, :, 1].astype(jnp.float32)
        spec_re = transform(forward_cos, signal_re) + transform(forward_sin, signal_im)
        spec_im = transform(forward_cos, signal_im) - transform(forward_sin, signal_re)
        return (spec_re, spec_im)

    lesser_re, lesser_im = spectrum(lesser)
    greater_re, greater_im = spectrum(greater)
    cross_re = lesser_re * greater_re + lesser_im * greater_im
    cross_im = lesser_im * greater_re - lesser_re * greater_im
    corr_re = (transform(inverse_cos, cross_re) - transform(inverse_sin, cross_im)) / length
    corr_im = (transform(inverse_cos, cross_im) + transform(inverse_sin, cross_re)) / length
    factor = 1.0 / math.sqrt(energies)
    polar_entries = jnp.stack([-corr_im * factor, corr_re * factor], axis=3).astype(jnp.bfloat16)
    return lax.all_to_all(polar_entries, "energy", split_axis=0, concat_axis=4, tiled=True)


def general(g_lesser, g_greater, v_diag, v_upper):
    local_rows = v_diag.shape[0]
    total_rows = local_rows * lax.axis_size("slab")
    first_row = lax.axis_index("slab") * local_rows
    inside = first_row + jnp.arange(local_rows, dtype=jnp.int32) < total_rows - 1
    inside = inside.astype(jnp.bfloat16)[:, None, None, None]
    coupling = jnp.stack([v_diag, v_upper * inside], axis=1)
    padded = extended(coupling, (("slab", 0),), 1)
    diag_below = padded[:-2, 0][None]
    diag_middle = padded[1:-1, 0][None]
    diag_above = padded[2:, 0][None]
    upper_below = padded[:-2, 1][None]
    upper_middle = padded[1:-1, 1][None]
    upper_above = padded[2:, 1][None]
    middle = correlate(
        (
            lax.all_to_all(g_lesser, "energy", split_axis=4, concat_axis=0, tiled=True),
            lax.all_to_all(g_greater, "energy", split_axis=4, concat_axis=0, tiled=True),
        )
    )
    toward_above_y = complex_product(middle[:, :, 1], upper_middle) + complex_product(
        middle[:, :, 2], diag_above
    )
    toward_above_z = complex_product(middle[:, :, 2], upper_above)
    toward_below_y = complex_product(middle[:, :, 0], diag_below) + complex_product(
        middle[:, :, 1], upper_below, False, True
    )
    toward_below_z = (
        complex_product(middle[:, :, 0], upper_below)
        + complex_product(middle[:, :, 1], diag_middle)
        + complex_product(middle[:, :, 2], upper_middle, False, True)
    )
    sent_up = jnp.stack([toward_above_y, toward_above_z], axis=2).astype(jnp.bfloat16)
    sent_down = jnp.stack([toward_below_y, toward_below_z], axis=2).astype(jnp.bfloat16)
    arrived_below = passed_along(sent_up[:, -1:], "slab", 1)
    from_below = jnp.concatenate([arrived_below, sent_up[:, :-1]], axis=1)
    arrived_above = passed_along(sent_down[:, :1], "slab", -1)
    from_above = jnp.concatenate([sent_down[:, 1:], arrived_above], axis=1)
    below_y = from_below[:, :, 0]
    below_z = from_below[:, :, 1]
    above_y = from_above[:, :, 0]
    above_z = from_above[:, :, 1]
    middle_y = (
        complex_product(middle[:, :, 0], upper_below)
        + complex_product(middle[:, :, 1], diag_middle)
        + complex_product(middle[:, :, 2], upper_middle, False, True)
    ).astype(jnp.bfloat16)
    middle_z = (
        complex_product(middle[:, :, 1], upper_middle)
        + complex_product(middle[:, :, 2], diag_above)
    ).astype(jnp.bfloat16)
    w_diag = (
        complex_product(upper_below, below_y, True, False)
        + complex_product(diag_middle, middle_y)
        + complex_product(upper_middle, above_y)
    ).astype(jnp.bfloat16)
    w_upper = (
        complex_product(upper_below, below_z, True, False)
        + complex_product(diag_middle, middle_z)
        + complex_product(upper_middle, above_z)
    ).astype(jnp.bfloat16)
    return (w_diag, w_upper)


ON_CHIP = [(0, 1), (1, 0), (2, 3), (3, 2)]
RAW = [(2, 0), (3, 1)]
RAW_ONE = [(3, 1)]
PARTIAL = [(0, 2), (1, 3)]


def chunks_of(rows):
    if rows % 256:
        return ((0, rows),)
    unit = rows // 16
    sizes = (6 * unit, 5 * unit, 5 * unit)
    starts = (0, 6 * unit, 11 * unit)
    return tuple(zip(starts, sizes))


def whole(shape):
    return pl.BlockSpec(shape, lambda *_: (0,) * len(shape))


def rows_of(shape, start, size):
    block = tuple(pl.Element(size if at == 4 else n) for at, n in enumerate(shape))
    return pl.BlockSpec(block, lambda *_: (0, 0, 0, 0, start, 0))


def scalars():
    return pl.BlockSpec(memory_space=pltpu.SMEM)


def params():
    return pltpu.CompilerParams(vmem_limit_bytes=48 << 20)


def f32(value):
    return value.astype(jnp.float32)


def times_conj(left, right):
    left_re, left_im = f32(left[0]), f32(left[1])
    right_re, right_im = f32(right[0]), f32(right[1])
    return (left_re * right_re + left_im * right_im, left_im * right_re - left_re * right_im)


def added(first, second):
    return (first[0] + second[0], first[1] + second[1])


def partial_kernel(place, l_own, g_own, l_mate, g_mate, l_far, out):
    l_own, g_own, l_mate, g_mate = (r.at[0, 0] for r in (l_own, g_own, l_mate, g_mate))
    bands = l_own.shape[0]

    @pl.when(place[0] == 0)
    def _():
        for b in range(bands):
            total = added(times_conj(l_own[b], g_own[b]), times_conj(l_mate[b], g_mate[b]))
            out[b, 0] = total[0].astype(out.dtype)
            out[b, 1] = total[1].astype(out.dtype)

    @pl.when(place[0] == 1)
    def _():
        for b in range(bands):
            total = added(times_conj(l_own[b], g_mate[b]), times_conj(l_far[b], g_own[b]))
            out[b, 0] = total[0].astype(out.dtype)
            out[b, 1] = total[1].astype(out.dtype)


def polar_kernel(factor, place, l_own, g_own, l_mate, g_mate, g_far, g_far_mate, l_far, arrived,
                 w_m1, w_0, w_1, w_2, near, far, own, polar):
    l_own, g_own, l_mate, g_mate = (r.at[0, 0] for r in (l_own, g_own, l_mate, g_mate))
    bands, _, rows, width = l_own.shape

    def put(b, total):
        re = (-total[1] * factor).astype(polar.dtype)
        im = (total[0] * factor).astype(polar.dtype)
        polar[b, :rows, :width] = re
        polar[b, rows:, :width] = im
        polar[b, :rows, width:] = -im
        polar[b, rows:, width:] = re

    @pl.when(place[0] == 0)
    def _():
        for b in range(bands):
            put(b, added(times_conj(l_own[b], g_far[b]), times_conj(l_mate[b], g_far_mate[b])))

    @pl.when(place[0] == 1)
    def _():
        for b in range(bands):
            total = added(times_conj(l_mate[b], g_own[b]), times_conj(l_own[b], g_far_mate[b]))
            put(b, added(total, times_conj(l_far[b], g_far[b])))

    @pl.when(place[0] == 2)
    def _():
        for b in range(bands):
            total = added(times_conj(l_own[b], g_own[b]), times_conj(l_mate[b], g_mate[b]))
            put(b, added(total, (f32(arrived[b, 0]), f32(arrived[b, 1]))))

    @pl.when(place[0] == 3)
    def _():
        for b in range(bands):
            total = times_conj(l_own[b], g_mate[b])
            put(b, added(total, (f32(arrived[b, 0]), f32(arrived[b, 1]))))

    def product(bands_used, weights):
        total = None
        for at, b in enumerate(bands_used):
            term = jnp.dot(
                polar[b],
                weights[at * 2 * width : (at + 1) * 2 * width, :],
                preferred_element_type=jnp.float32,
            )
            total = term if total is None else total + term
        return total.astype(near.dtype).reshape(2, rows, width)

    t_0 = product((0, 1, 2), w_0)
    t_1 = product((1, 2), w_1)
    t_m1 = product((0, 1), w_m1)
    t_2 = product((2,), w_2)
    own[0] = t_0
    own[1] = t_1

    @pl.when(place[1] == 0)
    def _():
        near[0] = t_1
        near[1] = t_2
        far[0] = t_m1
        far[1] = t_0

    @pl.when(place[1] == 1)
    def _():
        near[0] = t_m1
        near[1] = t_0
        far[0] = t_1
        far[1] = t_2


def coupling_kernel(place, diag, upper, near, near_mate, far, far_mate,
                    w_m1, w_0, w_1, w_2, left):
    width = diag.shape[-1]
    core = place[2]
    even = place[1] == 0

    def adjoint(block):
        return (block[0].T, -(block[1].T))

    def put(target, at, block):
        target[at * 2 * width : at * 2 * width + width, :] = block[0]
        target[at * 2 * width + width : (at + 1) * 2 * width, :] = block[1]

    def put_left(at, block):
        base = at * 2 * width
        left[:width, base : base + width] = block[0]
        left[width:, base : base + width] = block[1]
        left[:width, base + width : base + 2 * width] = -block[1]
        left[width:, base + width : base + 2 * width] = block[0]

    def work(diag_near, upper_near, diag_far, upper_far):
        own = (upper[0], upper[1])
        own_adjoint = adjoint(own)
        put(w_0, 1, diag)
        put(w_0, 2, own_adjoint)
        put(w_1, 0, own)
        put_left(1, (diag[0], diag[1]))

        def sided(diag_below, upper_below, diag_above, upper_above, below_at, above_at):
            below = (upper_below[0], upper_below[1])
            below_adjoint = adjoint(below)
            put(w_m1, 0, diag_below)
            put(w_m1, 1, below_adjoint)
            put(w_0, 0, below)
            put(w_1, 1, diag_above)
            put(w_2, 0, upper_above)
            put_left(below_at, below_adjoint)
            put_left(above_at, own)

        @pl.when(even)
        def _():
            sided(diag_far, upper_far, diag_near, upper_near, 2, 0)

        @pl.when(jnp.logical_not(even))
        def _():
            sided(diag_near, upper_near, diag_far, upper_far, 0, 2)

    @pl.when(core == 0)
    def _():
        work(near, near_mate, far, far_mate)

    @pl.when(core == 1)
    def _():
        work(near_mate, near, far_mate, far)


def final_kernel(count, *refs):
    own, near, far = refs[:count], refs[count : 2 * count], refs[2 * count : 3 * count]
    left, w_diag, w_upper, gathered, sems = refs[3 * count :]
    width = w_diag.shape[-1]
    copies = []
    for place, group in enumerate((near, own, far)):
        start = 0
        for at, piece in enumerate(group):
            size = piece.shape[2]
            copy = pltpu.make_async_copy(
                piece,
                gathered.at[place, :, :, start : start + size],
                sems.at[place, at],
            )
            copy.start()
            copies.append(copy)
            start += size
    for copy in copies:
        copy.wait()
    for index, out in enumerate((w_diag, w_upper)):
        total = None
        for place in range(3):
            term = jnp.dot(
                left[:, place * 2 * width : (place + 1) * 2 * width],
                gathered[place, index].reshape(2 * width, width),
                preferred_element_type=jnp.float32,
            )
            total = term if total is None else total + term
        out[...] = total.astype(out.dtype).reshape(2, width, width)


def exchanged(g_lesser, g_greater, v_diag, v_upper):
    bf16 = jnp.bfloat16
    energies = lax.axis_size("energy")
    slabs = lax.axis_size("slab")
    bands, width = g_lesser.shape[2], g_lesser.shape[5]
    energy = lax.axis_index("energy")
    slab = lax.axis_index("slab")
    core = energy % 2
    place = jnp.stack([energy, slab % 2, core]).astype(jnp.int32)
    near_pairs = [(i, i ^ 1) for i in range(slabs)]
    far_pairs = [(i, i + 1) for i in range(1, slabs - 1, 2)]
    far_pairs = far_pairs + [(j, i) for i, j in far_pairs]

    l_own, g_own = g_lesser, g_greater
    l_mate = lax.ppermute(l_own, "energy", ON_CHIP)
    g_mate = lax.ppermute(g_own, "energy", ON_CHIP)

    upper = jnp.where(slab == slabs - 1, jnp.zeros_like(v_upper), v_upper)[0]
    diag = v_diag[0]
    sent = jnp.where(core == 0, diag, upper)
    v_near = lax.ppermute(sent, "slab", near_pairs)
    v_far = lax.ppermute(sent, "slab", far_pairs)
    v_near_mate = lax.ppermute(v_near, "energy", ON_CHIP)
    v_far_mate = lax.ppermute(v_far, "energy", ON_CHIP)
    square = (2, width, width)
    right = [
        jax.ShapeDtypeStruct((2 * width * n, width), bf16) for n in (2, 3, 2, 1)
    ]
    *rights, left = pl.pallas_call(
        coupling_kernel,
        out_shape=(*right, jax.ShapeDtypeStruct((2 * width, 6 * width), bf16)),
        in_specs=[scalars()] + [whole(square)] * 6,
        out_specs=tuple(whole(r.shape) for r in right) + (whole((2 * width, 6 * width)),),
        compiler_params=params(),
        grid=(1,),
        name="coupling",
    )(place, diag, upper, v_near, v_near_mate, v_far, v_far_mate)

    owns, nears, fars = [], [], []
    for start, size in chunks_of(width):
        def cut(value):
            return lax.slice_in_dim(value, start, start + size, axis=4)

        piece = (bands, 2, size, width)
        raw_g = lax.ppermute(cut(g_own), "energy", RAW).reshape(piece)
        raw_l = lax.ppermute(cut(l_mate), "energy", RAW_ONE).reshape(piece)
        rows = rows_of(g_own.shape, start, size)
        partial = pl.pallas_call(
            partial_kernel,
            out_shape=jax.ShapeDtypeStruct(piece, bf16),
            in_specs=[scalars()] + [rows] * 4 + [whole(piece)],
            out_specs=whole(piece),
            compiler_params=params(),
            grid=(1,),
        name="partial",
        )(place, l_own, g_own, l_mate, g_mate, raw_l)
        arrived = lax.ppermute(partial, "energy", PARTIAL)
        raw_g_mate = lax.ppermute(raw_g, "energy", ON_CHIP)
        term = (2, 2, size, width)
        near, far, own = pl.pallas_call(
            lambda *refs: polar_kernel(1.0 / math.sqrt(energies), *refs),
            out_shape=(jax.ShapeDtypeStruct(term, bf16),) * 3,
            in_specs=[scalars()]
            + [rows] * 4
            + [whole(piece)] * 4
            + [whole(r.shape) for r in right],
            out_specs=(whole(term),) * 3,
            scratch_shapes=[pltpu.VMEM((bands, 2 * size, 2 * width), bf16)],
            compiler_params=params(),
            grid=(1,),
        name="polar",
        )(place, l_own, g_own, l_mate, g_mate, raw_g, raw_g_mate, raw_l, arrived, *rights)
        nears.append(lax.ppermute(near, "slab", near_pairs))
        fars.append(lax.ppermute(far, "slab", far_pairs))
        owns.append(own)

    count = len(owns)
    anywhere = pl.BlockSpec(memory_space=pl.ANY)
    w_diag, w_upper = pl.pallas_call(
        lambda *refs: final_kernel(count, *refs),
        out_shape=(jax.ShapeDtypeStruct(square, bf16),) * 2,
        in_specs=[anywhere] * (3 * count) + [whole((2 * width, 6 * width))],
        out_specs=(whole(square),) * 2,
        scratch_shapes=[
            pltpu.VMEM((3, 2, 2, width, width), bf16),
            pltpu.SemaphoreType.DMA((3, count)),
        ],
        compiler_params=params(),
        grid=(1,),
        name="final",
    )(*owns, *nears, *fars, left)
    shape = (1, 1) + square
    return w_diag.reshape(shape), w_upper.reshape(shape)


def per_device(g_lesser, g_greater, v_diag, v_upper):
    paired = lax.axis_size("energy") == 4 and lax.axis_size("slab") % 2 == 0
    if paired and g_lesser.shape[0] == 1 and v_diag.shape[0] == 1:
        return exchanged(g_lesser, g_greater, v_diag, v_upper)
    return general(g_lesser, g_greater, v_diag, v_upper)


def solution(mesh):
    placed = (
        P("energy", "slab", None, None, None, None),
        P("energy", "slab", None, None, None, None),
        P("slab", None, None, None),
        P("slab", None, None, None),
    )
    return jax.shard_map(
        per_device,
        mesh=mesh,
        in_specs=placed,
        out_specs=(P("energy", "slab", None, None, None), P("energy", "slab", None, None, None)),
        check_vma=False,
    )
```

```python
import math

import jax
import jax.numpy as jnp
from jax import lax
from jax.experimental import pallas as pl
from jax.experimental.pallas import tpu as pltpu
from jax.sharding import PartitionSpec as P


def extended(shard, sides, width):
    for axis, dim in sides:
        count, length = (lax.axis_size(axis), shard.shape[dim])
        up = [(i, (i + 1) % count) for i in range(count - 1)]
        down = [(j, i) for i, j in up]
        last = lax.slice_in_dim(shard, length - width, length, axis=dim)
        initial = lax.slice_in_dim(shard, 0, width, axis=dim)
        before = lax.ppermute(last, axis, up)
        after = lax.ppermute(initial, axis, down)
        shard = jnp.concatenate([before, shard, after], axis=dim)
    return shard


def passed_along(value, axis, steps):
    count = lax.axis_size(axis)
    initial, last = (max(0, -steps), min(count, count - steps))
    return lax.ppermute(value, axis, [(source, source + steps) for source in range(initial, last)])


def complex_product(left_block, right_block, left_adjoint=False, right_adjoint=False):
    left_re = left_block[..., 0, :, :]
    left_im = left_block[..., 1, :, :]
    right_re = right_block[..., 0, :, :]
    right_im = right_block[..., 1, :, :]
    pattern = (
        ("...ji" if left_adjoint else "...ij")
        + ","
        + ("...kj" if right_adjoint else "...jk")
        + "->...ik"
    )

    def contract(first_part, second_part):
        return jnp.einsum(pattern, first_part, second_part, preferred_element_type=jnp.float32)

    left_sign = -1.0 if left_adjoint else 1.0
    right_sign = -1.0 if right_adjoint else 1.0
    real_part = contract(left_re, right_re) - left_sign * right_sign * contract(left_im, right_im)
    imag_part = right_sign * contract(left_re, right_im) + left_sign * contract(left_im, right_re)
    return jnp.stack([real_part, imag_part], axis=-3)


def transform(table, signal):
    return jnp.einsum("fn,n...->f...", table, signal, precision=lax.Precision.HIGH)


def correlate(pieces):
    lesser, greater = pieces
    energies = lesser.shape[0]
    length = 2 * energies
    frequency = jnp.arange(length, dtype=jnp.int32)
    energy_ids = jnp.arange(energies, dtype=jnp.int32)
    step_angle = 2.0 * math.pi / length
    forward_angle = (frequency[:, None] * energy_ids[None, :] % length).astype(
        jnp.float32
    ) * step_angle
    shifts = energy_ids - energies // 2
    inverse_angle = (shifts[:, None] * frequency[None, :] % length).astype(jnp.float32) * step_angle
    forward_cos = jnp.cos(forward_angle)
    forward_sin = jnp.sin(forward_angle)
    inverse_cos = jnp.cos(inverse_angle)
    inverse_sin = jnp.sin(inverse_angle)

    def spectrum(signal):
        signal_re = signal[:, :, :, 0].astype(jnp.float32)
        signal_im = signal[:, :, :, 1].astype(jnp.float32)
        spec_re = transform(forward_cos, signal_re) + transform(forward_sin, signal_im)
        spec_im = transform(forward_cos, signal_im) - transform(forward_sin, signal_re)
        return (spec_re, spec_im)

    lesser_re, lesser_im = spectrum(lesser)
    greater_re, greater_im = spectrum(greater)
    cross_re = lesser_re * greater_re + lesser_im * greater_im
    cross_im = lesser_im * greater_re - lesser_re * greater_im
    corr_re = (transform(inverse_cos, cross_re) - transform(inverse_sin, cross_im)) / length
    corr_im = (transform(inverse_cos, cross_im) + transform(inverse_sin, cross_re)) / length
    factor = 1.0 / math.sqrt(energies)
    polar_entries = jnp.stack([-corr_im * factor, corr_re * factor], axis=3).astype(jnp.bfloat16)
    return lax.all_to_all(polar_entries, "energy", split_axis=0, concat_axis=4, tiled=True)


def general(g_lesser, g_greater, v_diag, v_upper):
    local_rows = v_diag.shape[0]
    total_rows = local_rows * lax.axis_size("slab")
    first_row = lax.axis_index("slab") * local_rows
    inside = first_row + jnp.arange(local_rows, dtype=jnp.int32) < total_rows - 1
    inside = inside.astype(jnp.bfloat16)[:, None, None, None]
    coupling = jnp.stack([v_diag, v_upper * inside], axis=1)
    padded = extended(coupling, (("slab", 0),), 1)
    diag_below = padded[:-2, 0][None]
    diag_middle = padded[1:-1, 0][None]
    diag_above = padded[2:, 0][None]
    upper_below = padded[:-2, 1][None]
    upper_middle = padded[1:-1, 1][None]
    upper_above = padded[2:, 1][None]
    middle = correlate(
        (
            lax.all_to_all(g_lesser, "energy", split_axis=4, concat_axis=0, tiled=True),
            lax.all_to_all(g_greater, "energy", split_axis=4, concat_axis=0, tiled=True),
        )
    )
    toward_above_y = complex_product(middle[:, :, 1], upper_middle) + complex_product(
        middle[:, :, 2], diag_above
    )
    toward_above_z = complex_product(middle[:, :, 2], upper_above)
    toward_below_y = complex_product(middle[:, :, 0], diag_below) + complex_product(
        middle[:, :, 1], upper_below, False, True
    )
    toward_below_z = (
        complex_product(middle[:, :, 0], upper_below)
        + complex_product(middle[:, :, 1], diag_middle)
        + complex_product(middle[:, :, 2], upper_middle, False, True)
    )
    sent_up = jnp.stack([toward_above_y, toward_above_z], axis=2).astype(jnp.bfloat16)
    sent_down = jnp.stack([toward_below_y, toward_below_z], axis=2).astype(jnp.bfloat16)
    arrived_below = passed_along(sent_up[:, -1:], "slab", 1)
    from_below = jnp.concatenate([arrived_below, sent_up[:, :-1]], axis=1)
    arrived_above = passed_along(sent_down[:, :1], "slab", -1)
    from_above = jnp.concatenate([sent_down[:, 1:], arrived_above], axis=1)
    below_y = from_below[:, :, 0]
    below_z = from_below[:, :, 1]
    above_y = from_above[:, :, 0]
    above_z = from_above[:, :, 1]
    middle_y = (
        complex_product(middle[:, :, 0], upper_below)
        + complex_product(middle[:, :, 1], diag_middle)
        + complex_product(middle[:, :, 2], upper_middle, False, True)
    ).astype(jnp.bfloat16)
    middle_z = (
        complex_product(middle[:, :, 1], upper_middle)
        + complex_product(middle[:, :, 2], diag_above)
    ).astype(jnp.bfloat16)
    w_diag = (
        complex_product(upper_below, below_y, True, False)
        + complex_product(diag_middle, middle_y)
        + complex_product(upper_middle, above_y)
    ).astype(jnp.bfloat16)
    w_upper = (
        complex_product(upper_below, below_z, True, False)
        + complex_product(diag_middle, middle_z)
        + complex_product(upper_middle, above_z)
    ).astype(jnp.bfloat16)
    return (w_diag, w_upper)


ON_CHIP = [(0, 1), (1, 0), (2, 3), (3, 2)]
ACROSS = [(0, 2), (2, 0), (1, 3), (3, 1)]
SHARES = (3, 3, 2)


def chunks_of(rows):
    unit = rows // 8
    if rows % 256:
        return ((0, rows),)
    start, found = (0, [])
    for share in SHARES:
        found.append((start, share * unit))
        start += share * unit
    return tuple(found)


def whole(shape):
    return pl.BlockSpec(shape, lambda *_: (0,) * len(shape))


def rows_of(shape, start, size):
    block = tuple(pl.Element(size if at == 4 else n) for at, n in enumerate(shape))
    return pl.BlockSpec(block, lambda *_: (0, 0, 0, 0, start, 0))


def scalars():
    return pl.BlockSpec(memory_space=pltpu.SMEM)


def params():
    return pltpu.CompilerParams(vmem_limit_bytes=48 << 20)


def f32(value):
    return value.astype(jnp.float32)


def times_conj(left, right):
    left_re, left_im = f32(left[0]), f32(left[1])
    right_re, right_im = f32(right[0]), f32(right[1])
    return (left_re * right_re + left_im * right_im, left_im * right_re - left_re * right_im)


def added(first, second):
    return (first[0] + second[0], first[1] + second[1])


def pack_kernel(place, l_own, g_own, l_mate, g_mate, out):
    l_own, g_own, l_mate, g_mate = (r.at[0, 0] for r in (l_own, g_own, l_mate, g_mate))
    rows = l_own.shape[2]
    half = rows // 2

    def put(b, total, start=0):
        out[b, 0, start : start + total[0].shape[0]] = total[0].astype(out.dtype)
        out[b, 1, start : start + total[1].shape[0]] = total[1].astype(out.dtype)

    for b in range(l_own.shape[0]):

        @pl.when(place[0] == 0)
        def _():
            own = times_conj(l_own[b], g_own[b])
            put(b, added(own, times_conj(l_mate[b], g_mate[b])))
            out[b, :, rows:] = g_mate[b, :, :half]

        @pl.when(place[0] == 1)
        def _():
            put(b, times_conj(l_own[b], g_mate[b]))
            out[b, :, rows:] = g_own[b, :, half:]

        @pl.when(place[0] == 2)
        def _():
            out[b, :, :rows] = g_own[b]
            put(b, times_conj(l_own[b, :, :half], g_mate[b, :, :half]), rows)

        @pl.when(place[0] == 3)
        def _():
            out[b, :, :rows] = g_own[b]
            put(b, times_conj(l_mate[b, :, half:], g_own[b, :, half:]), rows)


def polar_kernel(factor, place, l_own, g_own, l_mate, g_mate, arrived, beside,
                 w_m1, w_0, w_1, w_2, near, far, own, polar):
    l_own, g_own, l_mate, g_mate = (r.at[0, 0] for r in (l_own, g_own, l_mate, g_mate))
    bands, _, rows, width = l_own.shape
    half = rows // 2

    def put(b, total, start=0):
        size = total[0].shape[0]
        re = (-total[1] * factor).astype(polar.dtype)
        im = (total[0] * factor).astype(polar.dtype)
        polar[b, start : start + size, :width] = re
        polar[b, rows + start : rows + start + size, :width] = im
        polar[b, start : start + size, width:] = -im
        polar[b, rows + start : rows + start + size, width:] = re

    def two(first, second):
        return added(times_conj(*first), times_conj(*second))

    def plus(total, third):
        return added(total, (f32(third[0]), f32(third[1])))

    halves = ((0, half, beside), (half, rows, arrived))
    for b in range(bands):

        @pl.when(place[0] == 0)
        def _():
            put(b, two((l_own[b], arrived[b, :, :rows]), (l_mate[b], beside[b, :, :rows])))

        @pl.when(place[0] == 1)
        def _():
            for low, high, extra in halves:
                cut = (b, slice(None), slice(low, high))
                total = two((l_mate[cut], g_own[cut]), (l_own[cut], beside[cut]))
                put(b, plus(total, extra[b, :, rows:]), low)

        @pl.when(place[0] == 2)
        def _():
            total = two((l_own[b], g_own[b]), (l_mate[b], g_mate[b]))
            put(b, plus(total, arrived[b, :, :rows]))

        @pl.when(place[0] == 3)
        def _():
            for low, high, extra in halves:
                cut = (b, slice(None), slice(low, high))
                total = two((l_mate[cut], extra[b, :, rows:]), (l_own[cut], g_mate[cut]))
                put(b, plus(total, arrived[cut]), low)

    def product(bands_used, weights):
        total = None
        for at, b in enumerate(bands_used):
            term = jnp.dot(
                polar[b],
                weights[at * 2 * width : (at + 1) * 2 * width, :],
                preferred_element_type=jnp.float32,
            )
            total = term if total is None else total + term
        return total.astype(near.dtype).reshape(2, rows, width)

    t_0 = product((0, 1, 2), w_0)
    t_1 = product((1, 2), w_1)
    t_m1 = product((0, 1), w_m1)
    t_2 = product((2,), w_2)
    own[0] = t_0
    own[1] = t_1

    @pl.when(place[1] == 0)
    def _():
        near[0] = t_1
        near[1] = t_2
        far[0] = t_m1
        far[1] = t_0

    @pl.when(place[1] == 1)
    def _():
        near[0] = t_m1
        near[1] = t_0
        far[0] = t_1
        far[1] = t_2


def coupling_kernel(place, diag, upper, near, near_mate, far, far_mate,
                    w_m1, w_0, w_1, w_2, left):
    width = diag.shape[-1]
    core = place[2]
    even = place[1] == 0

    own_kept = (place[3] == 0).astype(diag.dtype)
    above_kept = (place[4] == 0).astype(diag.dtype)

    def kept(block, factor):
        return (block[0] * factor, block[1] * factor)

    def adjoint(block):
        return (block[0].T, -(block[1].T))

    def put(target, at, block):
        target[at * 2 * width : at * 2 * width + width, :] = block[0]
        target[at * 2 * width + width : (at + 1) * 2 * width, :] = block[1]

    def put_left(at, block):
        base = at * 2 * width
        left[:width, base : base + width] = block[0]
        left[width:, base : base + width] = block[1]
        left[:width, base + width : base + 2 * width] = -block[1]
        left[width:, base + width : base + 2 * width] = block[0]

    def work(diag_near, upper_near, diag_far, upper_far):
        own = kept(upper, own_kept)
        own_adjoint = adjoint(own)
        put(w_0, 1, diag)
        put(w_0, 2, own_adjoint)
        put(w_1, 0, own)
        put_left(1, (diag[0], diag[1]))

        def sided(diag_below, upper_below, diag_above, upper_above, below_at, above_at):
            below = (upper_below[0], upper_below[1])
            below_adjoint = adjoint(below)
            put(w_m1, 0, diag_below)
            put(w_m1, 1, below_adjoint)
            put(w_0, 0, below)
            put(w_1, 1, diag_above)
            put(w_2, 0, kept(upper_above, above_kept))
            put_left(below_at, below_adjoint)
            put_left(above_at, own)

        @pl.when(even)
        def _():
            sided(diag_far, upper_far, diag_near, upper_near, 2, 0)

        @pl.when(jnp.logical_not(even))
        def _():
            sided(diag_near, upper_near, diag_far, upper_far, 0, 2)

    @pl.when(core == 0)
    def _():
        work(near, near_mate, far, far_mate)

    @pl.when(core == 1)
    def _():
        work(near_mate, near, far_mate, far)


def final_kernel(count, *refs):
    own, near, far = refs[:count], refs[count : 2 * count], refs[2 * count : 3 * count]
    left, w_diag, w_upper, gathered, sems = refs[3 * count :]
    width = w_diag.shape[-1]
    copies = []
    for place, group in enumerate((near, own, far)):
        start = 0
        for at, piece in enumerate(group):
            size = piece.shape[2]
            copy = pltpu.make_async_copy(
                piece,
                gathered.at[place, :, :, start : start + size],
                sems.at[place, at],
            )
            copy.start()
            copies.append(copy)
            start += size
    for copy in copies:
        copy.wait()
    for index, out in enumerate((w_diag, w_upper)):
        total = None
        for place in range(3):
            term = jnp.dot(
                left[:, place * 2 * width : (place + 1) * 2 * width],
                gathered[place, index].reshape(2 * width, width),
                preferred_element_type=jnp.float32,
            )
            total = term if total is None else total + term
        out[...] = total.astype(out.dtype).reshape(2, width, width)


def called(kernel, *args, **kwargs):
    return pl.pallas_call(kernel, grid=(1,), compiler_params=params(), **kwargs)(*args)


def exchanged(g_lesser, g_greater, v_diag, v_upper):
    bf16 = jnp.bfloat16
    energies = lax.axis_size("energy")
    slabs = lax.axis_size("slab")
    bands, width = g_lesser.shape[2], g_lesser.shape[5]
    energy = lax.axis_index("energy")
    slab = lax.axis_index("slab")
    core = energy % 2
    place = jnp.stack([energy, slab % 2, core, slab == slabs - 1, slab == slabs - 2])
    place = place.astype(jnp.int32)
    near_pairs = [(i, i ^ 1) for i in range(slabs)]
    far_pairs = [(i, i + 1) for i in range(1, slabs - 1, 2)]
    far_pairs = far_pairs + [(j, i) for i, j in far_pairs]
    chunks = chunks_of(width)

    l_own, g_own = g_lesser, g_greater
    l_mate = lax.ppermute(l_own, "energy", ON_CHIP)
    g_mate = lax.ppermute(g_own, "energy", ON_CHIP)

    diag, upper = v_diag[0], v_upper[0]
    sent = jnp.where(core == 0, diag, upper)
    v_near = lax.ppermute(sent, "slab", near_pairs)
    v_far = lax.ppermute(sent, "slab", far_pairs)
    v_near_mate = lax.ppermute(v_near, "energy", ON_CHIP)
    v_far_mate = lax.ppermute(v_far, "energy", ON_CHIP)
    square = (2, width, width)
    right = [jax.ShapeDtypeStruct((2 * width * n, width), bf16) for n in (2, 3, 2, 1)]
    *rights, left = called(
        coupling_kernel,
        place, diag, upper, v_near, v_near_mate, v_far, v_far_mate,
        out_shape=(*right, jax.ShapeDtypeStruct((2 * width, 6 * width), bf16)),
        in_specs=[scalars()] + [whole(square)] * 6,
        out_specs=tuple(whole(r.shape) for r in right) + (whole((2 * width, 6 * width)),),
    )

    owns, nears, fars = [], [], []
    for start, size in chunks:
        payload = (bands, 2, size + size // 2, width)
        rows = rows_of(g_own.shape, start, size)
        packed = called(
            pack_kernel,
            place, l_own, g_own, l_mate, g_mate,
            out_shape=jax.ShapeDtypeStruct(payload, bf16),
            in_specs=[scalars()] + [rows] * 4,
            out_specs=whole(payload),
        )
        arrived = lax.ppermute(packed, "energy", ACROSS)
        beside = lax.ppermute(arrived, "energy", ON_CHIP)
        term = (2, 2, size, width)
        near, far, own = called(
            lambda *refs: polar_kernel(1.0 / math.sqrt(energies), *refs),
            place, l_own, g_own, l_mate, g_mate, arrived, beside, *rights,
            out_shape=(jax.ShapeDtypeStruct(term, bf16),) * 3,
            in_specs=[scalars()]
            + [rows] * 4
            + [whole(payload)] * 2
            + [whole(r.shape) for r in right],
            out_specs=(whole(term),) * 3,
            scratch_shapes=[pltpu.VMEM((bands, 2 * size, 2 * width), bf16)],
        )
        nears.append(lax.ppermute(near, "slab", near_pairs))
        fars.append(lax.ppermute(far, "slab", far_pairs))
        owns.append(own)

    count = len(owns)
    anywhere = pl.BlockSpec(memory_space=pl.ANY)
    w_diag, w_upper = called(
        lambda *refs: final_kernel(count, *refs),
        *owns, *nears, *fars, left,
        out_shape=(jax.ShapeDtypeStruct(square, bf16),) * 2,
        in_specs=[anywhere] * (3 * count) + [whole((2 * width, 6 * width))],
        out_specs=(whole(square),) * 2,
        scratch_shapes=[
            pltpu.VMEM((3, 2, 2, width, width), bf16),
            pltpu.SemaphoreType.DMA((3, count)),
        ],
    )
    shape = (1, 1) + square
    return w_diag.reshape(shape), w_upper.reshape(shape)


def fast(mesh):
    return mesh.shape["energy"] == 4 and mesh.shape["slab"] % 2 == 0


def per_device(g_lesser, g_greater, v_diag, v_upper):
    return exchanged(g_lesser, g_greater, v_diag, v_upper)


def solution(mesh):
    placed = (
        P("energy", "slab", None, None, None, None),
        P("energy", "slab", None, None, None, None),
        P("slab", None, None, None),
        P("slab", None, None, None),
    )
    quick = fast(mesh)
    return jax.shard_map(
        per_device if quick else general,
        mesh=mesh,
        in_specs=placed,
        out_specs=(P("energy", "slab", None, None, None), P("energy", "slab", None, None, None)),
        check_vma=False,
    )
```
